32 devices in a mesh: grp: 2 (over y), row: 8 (over z, x), col: 2 (over core).
Axes of the slice: x: 2, y: 2, z: 4, core: 2. Of those that a mesh axis runs over, the one named last changes fastest.
Arguments:
- grad_out: bfloat16 [1024, 8192], P(('grp', 'row'), 'col'), parts along dimension 0, may hold values from -6 to 6
- hidden_act: bfloat16 [1024, 22016], P(('grp', 'col'), 'row'), parts along dimension 0, may hold values from -6 to 6
- down_weight: bfloat16 [22016, 8192], P('row', 'col'), may hold values from -0.0390625 to 0.0390625
- proj_in: bfloat16 [22016, 64], P('row'), may hold values from -0.0390625 to 0.0390625
- proj_out: bfloat16 [8192, 64], P('col'), may hold values from -0.0625 to 0.0625
- queries: bfloat16 [128, 4096], P('row', 'col'), may hold values from -0.01171875 to 0.01171875
- example_ids: int32 [1024], P(('grp', 'row')), parts along dimension 0, may hold values from 0 to 7, never falling along the last dimension, each value on 1 to 128 neighbouring positions
Outputs:
- grad_hidden: bfloat16 [1024, 22016], P(('grp', 'col'), 'row'), parts along dimension 0
- weight_grad: bfloat16 [44032, 8192], P(('grp', 'row'), 'col'), parts along dimension 0
- scores: float32 [128, 16], P(('row', 'col'), 'grp'), parts along dimension 1
The draws below stay inside these ranges and needn't reach their ends.
There are 2 independent parts, one for each index of `grp`. The reference program is written for one: setup_inputs(seed, part) draws one part's arguments, and reference() takes and returns one part's arrays. A program takes and returns all parts, laid end to end along the dimension named above; an argument that names none is the same for every part. Nothing has to cross between parts.
Inputs may be any that keep to these rules, and one draw needn't show every extreme that they name: `example_ids`: never falling along the tokens; each example holds 1 to 128 tokens, one exactly 128.
All inputs are finite; a program needn't handle non-finite values.
Results may differ from the reference program's by a relative error of at most 0.001.
Values may be sent and summed in bfloat16 or wider, within the bound.
A program may use at most 192 MiB of HBM per device.

```python
import math
import jax
import jax.numpy as jnp
import numpy as np
from jax import lax

D = 8192
FF = 22016
RANK = 64
TOK = 512
EXAMPLES = 8
MOST = 128
NQ = 128
K = 4096


def levels(stream_key, dims, cuts, least, largest):
    loudness = 1.0
    for axis_at, shards_of in cuts:
        draws = jax.random.uniform(jax.random.fold_in(jax.random.fold_in(stream_key, 6), axis_at), (shards_of,), jnp.float32, least / len(cuts), largest / len(cuts))
        loudness = loudness * jnp.repeat(jnp.exp(draws), dims[axis_at] // shards_of).reshape((-1,) + (1,) * (len(dims) - 1 - axis_at))
    return loudness


def length_profile(count, total, reach, lean):
    weights = [(1 << 20) // math.isqrt(rank ** lean) + 1 for rank in range(2, count + 1)]
    spare, counts = total - reach - (count - 1), [1] * (count - 1)
    while spare > 0:
        movable = [i for i in range(count - 1) if counts[i] < reach]
        pool, budget = sum([weights[i] for i in movable]), spare
        for i in movable:
            more = min(reach - counts[i], max(1, budget * weights[i] // pool), spare)
            counts[i] = counts[i] + more
            spare = spare - more
    return np.array([reach] + counts)


def ragged_sizes(key, amount, total, reach, slope):
    if amount == 2:
        one = jax.random.randint(key, (), max(1, total - reach), min(reach, total - 1) + 1)
        return jnp.stack([one, total - one])
    lengths = jnp.asarray(length_profile(amount, total, reach, slope), jnp.int32)
    pairs = (amount - 1) // 2
    source_of, taker = lengths[1:1 + 2 * pairs:2], lengths[2:2 + 2 * pairs:2]
    margin = jnp.minimum(source_of - 1, reach - taker)
    shifted = jax.random.randint(jax.random.fold_in(key, 1), (pairs,), 0, 1 << 20) % (margin + 1)
    lengths = lengths.at[1:1 + 2 * pairs:2].set(source_of - shifted).at[2:2 + 2 * pairs:2].set(taker + shifted)
    return lengths[jax.random.permutation(jax.random.fold_in(key, 2), amount)]


def centred(stream_key, shape, width, reach, split=(), kind=jnp.bfloat16):
    gain = levels(stream_key, shape, split, -0.22, 0.18) if split else 1.0
    result = jax.random.normal(stream_key, shape, jnp.float32) * width * gain
    return jnp.minimum(jnp.maximum(result, -reach), reach).astype(kind)


def setup_inputs(seed: int = 0, part: int = 0) -> dict:
    splits = jax.random.split(jax.random.key(seed), 8)
    own_keys = jax.random.split(jax.random.fold_in(splits[7], part), 8)
    grad_out = centred(own_keys[0], (TOK, D), 1.0, 6.0, ((0, 8), (1, 2)))
    hidden_act = centred(own_keys[1], (TOK, FF), 1.0, 6.0, ((0, 2), (1, 8)))
    down_weight = centred(splits[2], (FF, D), FF ** -0.5, 0.0390625, ((0, 8), (1, 2)))
    proj_in = centred(splits[3], (FF, RANK), FF ** -0.5, 0.0390625, ((0, 8),))
    proj_out = centred(splits[4], (D, RANK), D ** -0.5, 0.0625, ((0, 2),))
    queries = centred(splits[5], (NQ, K), (64 * K) ** -0.5, 0.01171875, ((0, 8), (1, 2)))
    example_ids = jnp.searchsorted(jnp.cumsum(ragged_sizes(own_keys[6], EXAMPLES, TOK, MOST, 1)), jnp.arange(TOK), side="right").astype(jnp.int32)
    return {"grad_out": grad_out, "hidden_act": hidden_act, "down_weight": down_weight, "proj_in": proj_in, "proj_out": proj_out, "queries": queries, "example_ids": example_ids}


def reference(grad_out, hidden_act, down_weight, proj_in, proj_out, queries, example_ids):
    grad_hidden = lax.dot_general(grad_out, down_weight, (((1,), (1,)), ((), ())), preferred_element_type=jnp.float32).astype(jnp.bfloat16)
    weight_grad = lax.dot_general(hidden_act, grad_out, (((0,), (0,)), ((), ())), preferred_element_type=jnp.float32).astype(jnp.bfloat16)
    in_factor = jnp.dot(hidden_act, proj_in, preferred_element_type=jnp.float32)
    out_factor = jnp.dot(grad_out, proj_out, preferred_element_type=jnp.float32)
    outer_terms = (in_factor[:, :, None] * out_factor[:, None, :]).reshape(in_factor.shape[0], -1)
    labels = jnp.arange(EXAMPLES, dtype=jnp.int32)
    onehot = (example_ids[None, :] == labels[:, None]).astype(jnp.float32)
    example_grad = jnp.dot(onehot, outer_terms, precision=lax.Precision.HIGHEST)
    scores = jnp.dot(queries.astype(jnp.float32), example_grad.T, precision=lax.Precision.HIGHEST)
    return (grad_hidden, weight_grad, scores)
```

```python
import jax
import jax.numpy as jnp
from jax import lax
from jax.experimental import pallas as pl
from jax.experimental.pallas import tpu as pltpu
from jax.sharding import PartitionSpec as P

EXAMPLES = 8
CHUNKS = 4


def swap(x, axis, bit):
    n = lax.axis_size(axis)
    return lax.ppermute(x, axis, [(i, i ^ bit) for i in range(n)])


def pair_order(own, other, index, axis):
    first = jnp.where(index == 0, own, other)
    second = jnp.where(index == 0, other, own)
    return jnp.concatenate([first, second], axis=axis)


def gather_rows(block):
    n = lax.axis_size("row")
    if n % 2 or n > 16:
        return lax.all_gather(block, "row", axis=0, tiled=True)
    outer = n // 2
    me = lax.axis_index("row")
    z, x = me // 2, me % 2
    held = [block]
    for k in range(1, outer):
        perm = [(i, ((i // 2 + k) % outer) * 2 + i % 2) for i in range(n)]
        held.append(lax.ppermute(block, "row", perm))
    mine = jnp.stack(held[::-1])
    theirs = swap(mine, "row", 1)
    both = pair_order(mine, theirs, x, 1)
    twice = jnp.concatenate([both, both], axis=0)
    rows = lax.dynamic_slice_in_dim(twice, outer - 1 - z, outer, 0)
    return rows.reshape((n * block.shape[0],) + block.shape[1:])


def sum_rows(x):
    n = lax.axis_size("row")
    if n & (n - 1):
        return lax.psum(x, "row")
    bit = 1
    while bit < n:
        x = x + swap(x, "row", bit)
        bit *= 2
    return x


def product_kernel(a_ref, b_ref, *refs):
    out_ref = refs[-1]
    out_ref[...] = jnp.dot(
        a_ref[...], b_ref[...], preferred_element_type=jnp.float32
    ).astype(out_ref.dtype)


def product_into(a, b, total, at, chunks):
    rows, depth = a.shape
    width = b.shape[1]
    tile = rows
    for parts in (8, 4, 2):
        if rows % (parts * 16) == 0:
            tile = rows // parts
            break
    in_specs = [
        pl.BlockSpec((tile, depth), lambda i: (i, 0)),
        pl.BlockSpec((depth, width), lambda i: (0, 0)),
    ]
    args = (a, b)
    aliases = {}
    if total is not None:
        in_specs.append(pl.BlockSpec(memory_space=pl.ANY))
        args = (a, b, total)
        aliases = {2: 0}
    return pl.pallas_call(
        product_kernel,
        grid=(rows // tile,),
        in_specs=in_specs,
        out_specs=pl.BlockSpec((tile, width), lambda i: (i, at)),
        out_shape=jax.ShapeDtypeStruct((rows, chunks * width), jnp.bfloat16),
        input_output_aliases=aliases,
        compiler_params=pltpu.CompilerParams(vmem_limit_bytes=24 << 20),
        cost_estimate=pl.CostEstimate(
            flops=2 * rows * depth * width,
            bytes_accessed=2 * (rows * depth + depth * width + rows * width),
            transcendentals=0,
        ),
    )(*args)


def body(grad_out, hidden_act, down_weight, proj_in, proj_out, queries, example_ids):
    f32 = jnp.float32
    col = lax.axis_index("col")
    half_rank = proj_in.shape[1] // lax.axis_size("col")

    width = grad_out.shape[1] // CHUNKS
    parts = [
        gather_rows(lax.slice_in_dim(grad_out, c * width, (c + 1) * width, axis=1))
        for c in range(CHUNKS)
    ]

    other_hidden = swap(hidden_act, "col", 1)
    full_hidden = pair_order(hidden_act, other_hidden, col, 0)
    hidden_t = full_hidden.T

    own_proj = lax.dynamic_slice_in_dim(proj_in, col * half_rank, half_rank, 1)
    in_factor = sum_rows(
        lax.dot_general(own_proj, full_hidden, (((0,), (1,)), ((), ())), preferred_element_type=f32)
    )

    out_own = lax.dot_general(
        proj_out, grad_out, (((0,), (1,)), ((), ())), preferred_element_type=f32
    ).T
    out_own = out_own + swap(out_own, "col", 1)
    packed = gather_rows(jnp.concatenate([out_own, example_ids[:, None].astype(f32)], axis=1))
    out_factor = packed[:, :-1]
    ids = packed[:, -1].astype(jnp.int32)
    labels = jnp.arange(EXAMPLES, dtype=jnp.int32)
    onehot = ids[None, :] == labels[:, None]
    masked = jnp.where(onehot[:, None, :], in_factor[None], 0.0)
    example_grads = jnp.dot(
        masked.reshape(EXAMPLES * half_rank, -1), out_factor, precision=lax.Precision.HIGHEST
    ).reshape(EXAMPLES, -1)
    values = lax.dot_general(
        queries.astype(f32), example_grads, (((1,), (1,)), ((), ())), precision=lax.Precision.HIGHEST
    )
    share = values.shape[0] // 2
    keep = lax.dynamic_slice_in_dim(values, col * share, share, 0)
    send = lax.dynamic_slice_in_dim(values, (1 - col) * share, share, 0)
    scores = keep + swap(send, "col", 1)

    total = None
    weight_grad = None
    for c in range(CHUNKS):
        weights = lax.slice_in_dim(down_weight, c * width, (c + 1) * width, axis=1)
        term = lax.dot_general(
            parts[c], weights, (((1,), (1,)), ((), ())), preferred_element_type=f32
        )
        total = term if total is None else total + term
        weight_grad = product_into(hidden_t, parts[c], weight_grad, c, CHUNKS)
    tokens = total.shape[0] // 2
    keep = lax.dynamic_slice_in_dim(total, col * tokens, tokens, 0)
    send = lax.dynamic_slice_in_dim(total, (1 - col) * tokens, tokens, 0)
    grad_hidden = (keep + swap(send, "col", 1)).astype(jnp.bfloat16)
    return (grad_hidden, weight_grad, scores)


def solution(mesh):
    return jax.shard_map(
        body,
        mesh=mesh,
        in_specs=(
            P(("grp", "row"), "col"),
            P(("grp", "col"), "row"),
            P("row", "col"),
            P("row", None),
            P("col", None),
            P("row", "col"),
            P(("grp", "row")),
        ),
        out_specs=(P(("grp", "col"), "row"), P(("grp", "row"), "col"), P(("row", "col"), "grp")),
        check_vma=False,
    )
```

```python
import functools

import jax
import jax.numpy as jnp
from jax import lax
from jax.experimental import pallas as pl
from jax.experimental.pallas import tpu as pltpu
from jax.sharding import PartitionSpec as P

EXAMPLES = 8
CHUNKS = 4
KERNEL_CHUNKS = 8


def swap(x, axis, bit):
    n = lax.axis_size(axis)
    return lax.ppermute(x, axis, [(i, i ^ bit) for i in range(n)])


def pair_order(own, other, index, axis):
    first = jnp.where(index == 0, own, other)
    second = jnp.where(index == 0, other, own)
    return jnp.concatenate([first, second], axis=axis)


def gather_rows(block):
    n = lax.axis_size("row")
    if n % 2 or n > 16:
        return lax.all_gather(block, "row", axis=0, tiled=True)
    outer = n // 2
    me = lax.axis_index("row")
    z, x = me // 2, me % 2
    held = [block]
    for k in range(1, outer):
        perm = [(i, ((i // 2 + k) % outer) * 2 + i % 2) for i in range(n)]
        held.append(lax.ppermute(block, "row", perm))
    mine = jnp.stack(held[::-1])
    theirs = swap(mine, "row", 1)
    both = pair_order(mine, theirs, x, 1)
    twice = jnp.concatenate([both, both], axis=0)
    rows = lax.dynamic_slice_in_dim(twice, outer - 1 - z, outer, 0)
    return rows.reshape((n * block.shape[0],) + block.shape[1:])


def sum_rows(x):
    n = lax.axis_size("row")
    if n & (n - 1):
        return lax.psum(x, "row")
    bit = 1
    while bit < n:
        x = x + swap(x, "row", bit)
        bit *= 2
    return x


def product_kernel(a_ref, b_ref, *refs):
    out_ref = refs[-1]
    out_ref[...] = jnp.dot(
        a_ref[...], b_ref[...], preferred_element_type=jnp.float32
    ).astype(out_ref.dtype)


def product_into(a, b, total, at, chunks):
    rows, depth = a.shape
    width = b.shape[1]
    tile = rows
    for parts in (8, 4, 2):
        if rows % (parts * 16) == 0:
            tile = rows // parts
            break
    in_specs = [
        pl.BlockSpec((tile, depth), lambda i: (i, 0)),
        pl.BlockSpec((depth, width), lambda i: (0, 0)),
    ]
    args = (a, b)
    aliases = {}
    if total is not None:
        in_specs.append(pl.BlockSpec(memory_space=pl.ANY))
        args = (a, b, total)
        aliases = {2: 0}
    return pl.pallas_call(
        product_kernel,
        grid=(rows // tile,),
        in_specs=in_specs,
        out_specs=pl.BlockSpec((tile, width), lambda i: (i, at)),
        out_shape=jax.ShapeDtypeStruct((rows, chunks * width), jnp.bfloat16),
        input_output_aliases=aliases,
        compiler_params=pltpu.CompilerParams(vmem_limit_bytes=24 << 20),
        cost_estimate=pl.CostEstimate(
            flops=2 * rows * depth * width,
            bytes_accessed=2 * (rows * depth + depth * width + rows * width),
            transcendentals=0,
        ),
    )(*args)


def plain_body(grad_out, hidden_act, down_weight, proj_in, proj_out, queries, example_ids):
    f32 = jnp.float32
    col = lax.axis_index("col")
    half_rank = proj_in.shape[1] // lax.axis_size("col")

    width = grad_out.shape[1] // CHUNKS
    parts = [
        gather_rows(lax.slice_in_dim(grad_out, c * width, (c + 1) * width, axis=1))
        for c in range(CHUNKS)
    ]

    other_hidden = swap(hidden_act, "col", 1)
    full_hidden = pair_order(hidden_act, other_hidden, col, 0)
    hidden_t = full_hidden.T

    own_proj = lax.dynamic_slice_in_dim(proj_in, col * half_rank, half_rank, 1)
    in_factor = sum_rows(
        lax.dot_general(own_proj, full_hidden, (((0,), (1,)), ((), ())), preferred_element_type=f32)
    )

    out_own = lax.dot_general(
        proj_out, grad_out, (((0,), (1,)), ((), ())), preferred_element_type=f32
    ).T
    out_own = out_own + swap(out_own, "col", 1)
    packed = gather_rows(jnp.concatenate([out_own, example_ids[:, None].astype(f32)], axis=1))
    out_factor = packed[:, :-1]
    ids = packed[:, -1].astype(jnp.int32)
    labels = jnp.arange(EXAMPLES, dtype=jnp.int32)
    onehot = ids[None, :] == labels[:, None]
    masked = jnp.where(onehot[:, None, :], in_factor[None], 0.0)
    example_grads = jnp.dot(
        masked.reshape(EXAMPLES * half_rank, -1), out_factor, precision=lax.Precision.HIGHEST
    ).reshape(EXAMPLES, -1)
    values = lax.dot_general(
        queries.astype(f32), example_grads, (((1,), (1,)), ((), ())), precision=lax.Precision.HIGHEST
    )
    share = values.shape[0] // 2
    keep = lax.dynamic_slice_in_dim(values, col * share, share, 0)
    send = lax.dynamic_slice_in_dim(values, (1 - col) * share, share, 0)
    scores = keep + swap(send, "col", 1)

    total = None
    weight_grad = None
    for c in range(CHUNKS):
        weights = lax.slice_in_dim(down_weight, c * width, (c + 1) * width, axis=1)
        term = lax.dot_general(
            parts[c], weights, (((1,), (1,)), ((), ())), preferred_element_type=f32
        )
        total = term if total is None else total + term
        weight_grad = product_into(hidden_t, parts[c], weight_grad, c, CHUNKS)
    tokens = total.shape[0] // 2
    keep = lax.dynamic_slice_in_dim(total, col * tokens, tokens, 0)
    send = lax.dynamic_slice_in_dim(total, (1 - col) * tokens, tokens, 0)
    grad_hidden = (keep + swap(send, "col", 1)).astype(jnp.bfloat16)
    return (grad_hidden, weight_grad, scores)


def tiling(rows):
    for parts in (4, 2):
        if rows % (parts * 16) == 0:
            return rows // parts
    return rows


def row_ids(z, x):
    return z * 2 + x


def gather_kernel(
    n, chunks, g_ref, h_ref, w_ref, p_ref, q_ref, ids_ref,
    gh_ref, gall_ref, ht_ref, in_ref, out_ref,
    gbuf, wbuf, hbuf, acc, rbuf, sums, rsum, outs, rout,
    z_send, z_recv, x_send, x_recv, w_sem, own_sem, all_sem, h_sem, ht_sem,
    a_send, a_recv, s_send, s_recv, o_send, o_recv,
):
    f32 = jnp.float32
    me = lax.axis_index("row")
    col = lax.axis_index("col")
    outer = n // 2
    z, x = me // 2, me % 2
    tok = g_ref.shape[0]
    width = g_ref.shape[1] // chunks
    rows, half = h_ref.shape
    tile = tiling(rows)
    tiles = rows // tile
    partner = {"row": row_ids(z, 1 - x)}
    twin = {"col": 1 - col}
    mesh_ids = pl.DeviceIdType.MESH

    def ahead(k):
        return {"row": row_ids((z + k) % outer, x)}

    barrier = pltpu.get_barrier_semaphore()
    peers = [partner, twin] + [ahead(k) for k in range(1, outer)]
    for peer in peers:
        pl.semaphore_signal(barrier, inc=1, device_id=peer, device_id_type=mesh_ids)
    pl.semaphore_wait(barrier, len(peers))

    def remote(src, dst, send, recv, device):
        return pltpu.make_async_remote_copy(
            src_ref=src, dst_ref=dst, send_sem=send, recv_sem=recv,
            device_id=device, device_id_type=mesh_ids,
        )

    def slot(c, owner):
        return gbuf.at[c, pl.ds(pl.multiple_of(owner * tok, tok), tok), :]

    hidden_own = pltpu.make_async_copy(h_ref, hbuf.at[col], h_sem.at[0])
    hidden_out = remote(h_ref, hbuf.at[col], h_sem.at[1], h_sem.at[2], twin)
    hidden_out.start()
    hidden_own.start()
    z_copies, x_copies, w_copies, own_copies = {}, {}, [], []
    for c in range(chunks):
        block = g_ref.at[:, c * width:(c + 1) * width]
        for k in range(1, outer):
            z_copies[c, k] = remote(
                block, slot(c, me), z_send.at[c, k], z_recv.at[c, k], ahead(k)
            )
            z_copies[c, k].start()
        x_copies[c, 0] = remote(block, slot(c, me), x_send.at[c, 0], x_recv.at[c, 0], partner)
        if c == 0:
            x_copies[c, 0].start()
        own_copies.append(pltpu.make_async_copy(block, slot(c, me), own_sem.at[c]))
        own_copies[c].start()
    for c in range(chunks):
        w_copies.append(
            pltpu.make_async_copy(
                w_ref.at[:, c * width:(c + 1) * width], wbuf.at[c], w_sem.at[c]
            )
        )
        w_copies[c].start()

    hidden_own.wait()
    hidden_out.wait()
    ht_copy = pltpu.make_async_copy(hbuf, ht_ref, ht_sem.at[0])
    ht_copy.start()
    rank = p_ref.shape[0]
    for h in range(2):
        sums[0, :rank, h * half:(h + 1) * half] = jnp.dot(
            p_ref[...], hbuf[h], preferred_element_type=f32
        )
    sums[0, rank:, :] = ids_ref[...]

    rounds = n.bit_length() - 1

    def round_copy(r):
        device = partner
        if r:
            bit = 1 << (r - 1)
            flipped = z + bit - 2 * bit * ((z // bit) % 2)
            device = {"row": row_ids(flipped, x)}
        return remote(sums.at[r], rsum.at[r], s_send.at[r], s_recv.at[r], device)

    round_copies = [round_copy(r) for r in range(rounds)]
    round_copies[0].start()

    def finish_round(r):
        round_copies[r].wait()
        total = sums[r] + rsum[r]
        if r + 1 < rounds:
            sums[r + 1] = total
            round_copies[r + 1].start()
        else:
            in_ref[...] = total

    outs[...] = jnp.zeros_like(outs)
    exchange = [
        remote(
            acc.at[1 - col, t * tile:(t + 1) * tile, :], rbuf.at[t * tile:(t + 1) * tile, :],
            a_send.at[t], a_recv.at[t], twin,
        )
        for t in range(tiles)
    ]
    out_copy = remote(outs, rout, o_send.at[0], o_recv.at[0], twin)
    all_copies = []

    def process(c):
        last = c == chunks - 1
        w_copies[c].wait()
        own_copies[c].wait()
        for k in range(outer):
            x_copies[c, k].wait_recv()
        all_copies.append(pltpu.make_async_copy(gbuf.at[c], gall_ref.at[c], all_sem.at[c]))
        all_copies[c].start()
        outs[...] += lax.dot_general(
            q_ref[:, c * width:(c + 1) * width], gbuf[c],
            (((1,), (1,)), ((), ())), preferred_element_type=f32,
        )
        if last:
            out_copy.start()

        for which in (1 - col, col):
            tokens = gbuf[c, pl.ds(pl.multiple_of(which * half, half), half), :]

            def one(t, carry, which=which, tokens=tokens):
                at = pl.ds(pl.multiple_of(t * tile, 16), tile)
                term = lax.dot_general(
                    wbuf[c, at, :], tokens, (((1,), (1,)), ((), ())), preferred_element_type=f32
                )
                if c:
                    term = term + acc[which, at, :]
                acc[which, at, :] = term
                return carry

            if last and which is not col:
                for t in range(tiles):
                    one(t, 0)
                    exchange[t].start()
            else:
                lax.fori_loop(0, tiles, one, 0)

    for c in range(chunks):
        if c:
            x_copies[c, 0].start()
        for k in range(1, outer):
            z_copies[c, k].wait_recv()
            landed = slot(c, row_ids((z + outer - k) % outer, x))
            x_copies[c, k] = remote(landed, landed, x_send.at[c, k], x_recv.at[c, k], partner)
            x_copies[c, k].start()
        if c:
            process(c - 1)
        if c < rounds:
            finish_round(c)
    process(chunks - 1)
    for r in range(chunks, rounds):
        finish_round(r)

    out_copy.wait()
    out_ref[...] = outs[...] + rout[...]
    for t in range(tiles):
        exchange[t].wait()
        at = slice(t * tile, (t + 1) * tile)
        gh_ref[at, :] = (acc[col, at, :] + rbuf[at, :]).astype(gh_ref.dtype)
    for c in range(chunks):
        for k in range(outer):
            x_copies[c, k].wait_send()
            if k:
                z_copies[c, k].wait_send()
        all_copies[c].wait()
    ht_copy.wait()


def weight_kernel(h_ref, g_ref, out_ref):
    half = h_ref.shape[2]
    total = jnp.dot(h_ref[0], g_ref[0, :half, :], preferred_element_type=jnp.float32)
    total += jnp.dot(h_ref[1], g_ref[0, half:, :], preferred_element_type=jnp.float32)
    out_ref[...] = total.astype(out_ref.dtype)


def body(grad_out, hidden_act, down_weight, proj_in, proj_out, queries, example_ids):
    f32, bf16 = jnp.float32, jnp.bfloat16
    n = lax.axis_size("row")
    tok, features = grad_out.shape
    half, rows = hidden_act.shape
    if n & (n - 1) or n < 4 or n > 16 or lax.axis_size("col") != 2 or features % (128 * KERNEL_CHUNKS):
        return plain_body(
            grad_out, hidden_act, down_weight, proj_in, proj_out, queries, example_ids
        )
    chunks = KERNEL_CHUNKS
    col, row = lax.axis_index("col"), lax.axis_index("row")
    width = features // chunks
    tokens = n * tok
    rank = proj_in.shape[1]
    half_rank = rank // 2
    outer = n // 2
    rounds = n.bit_length() - 1
    tile = tiling(rows)
    tiles = rows // tile
    own_proj = lax.dynamic_slice_in_dim(proj_in.T, col * half_rank, half_rank, 0)
    own_ids = lax.dynamic_update_slice(
        jnp.zeros((8, tokens), f32),
        jnp.broadcast_to(example_ids.astype(f32)[None], (8, tok)),
        (0, row * tok),
    )
    anywhere = pl.BlockSpec(memory_space=pl.ANY)
    vmem = pl.BlockSpec(memory_space=pltpu.VMEM)
    dma = pltpu.SemaphoreType.DMA
    packed = half_rank + 8
    gh_t, grads, hidden_t, in_sum, out_sum = pl.pallas_call(
        functools.partial(gather_kernel, n, chunks),
        out_shape=(
            jax.ShapeDtypeStruct((rows, half), bf16),
            jax.ShapeDtypeStruct((chunks, tokens, width), bf16),
            jax.ShapeDtypeStruct((2, rows, half), bf16),
            jax.ShapeDtypeStruct((packed, tokens), f32),
            jax.ShapeDtypeStruct((rank, tokens), f32),
        ),
        in_specs=[anywhere, anywhere, anywhere, vmem, vmem, vmem],
        out_specs=(vmem, anywhere, anywhere, vmem, vmem),
        scratch_shapes=[
            pltpu.VMEM((chunks, tokens, width), bf16),
            pltpu.VMEM((chunks, rows, width), bf16),
            pltpu.VMEM((2, rows, half), bf16),
            pltpu.VMEM((2, rows, half), f32),
            pltpu.VMEM((rows, half), f32),
            pltpu.VMEM((rounds, packed, tokens), f32),
            pltpu.VMEM((rounds, packed, tokens), f32),
            pltpu.VMEM((rank, tokens), f32),
            pltpu.VMEM((rank, tokens), f32),
            dma((chunks, outer)), dma((chunks, outer)),
            dma((chunks, outer)), dma((chunks, outer)),
            dma((chunks,)), dma((chunks,)), dma((chunks,)), dma((3,)), dma((1,)),
            dma((tiles,)), dma((tiles,)), dma((rounds,)), dma((rounds,)), dma((1,)), dma((1,)),
        ],
        compiler_params=pltpu.CompilerParams(
            collective_id=0, has_side_effects=True, vmem_limit_bytes=56 << 20
        ),
        name="gather",
    )(grad_out, hidden_act.T, down_weight, own_proj, proj_out.T, own_ids)

    in_factor = in_sum[:half_rank]
    ids = in_sum[half_rank].astype(jnp.int32)
    labels = jnp.arange(EXAMPLES, dtype=jnp.int32)
    onehot = ids[None, :] == labels[:, None]
    masked = jnp.where(onehot[:, None, :], in_factor[None], 0.0)
    example_grads = lax.dot_general(
        masked.reshape(EXAMPLES * half_rank, -1), out_sum, (((1,), (1,)), ((), ())),
        precision=lax.Precision.HIGHEST,
    ).reshape(EXAMPLES, -1)
    values = lax.dot_general(
        queries.astype(f32), example_grads, (((1,), (1,)), ((), ())), precision=lax.Precision.HIGHEST
    )
    share = values.shape[0] // 2
    keep = lax.dynamic_slice_in_dim(values, col * share, share, 0)
    send = lax.dynamic_slice_in_dim(values, (1 - col) * share, share, 0)
    scores = keep + swap(send, "col", 1)

    weight_grad = pl.pallas_call(
        weight_kernel,
        grid=(chunks, tiles),
        in_specs=[
            pl.BlockSpec((2, tile, half), lambda c, t: (0, t, 0)),
            pl.BlockSpec((1, tokens, width), lambda c, t: (c, 0, 0)),
        ],
        out_specs=pl.BlockSpec((tile, width), lambda c, t: (t, c)),
        out_shape=jax.ShapeDtypeStruct((rows, features), bf16),
        compiler_params=pltpu.CompilerParams(vmem_limit_bytes=24 << 20),
        cost_estimate=pl.CostEstimate(
            flops=2 * rows * tokens * features,
            bytes_accessed=2 * (rows * tokens + tokens * features + rows * features),
            transcendentals=0,
        ),
        name="weight",
    )(hidden_t, grads)
    return (gh_t.T, weight_grad, scores)


def solution(mesh):
    return jax.shard_map(
        body,
        mesh=mesh,
        in_specs=(
            P(("grp", "row"), "col"),
            P(("grp", "col"), "row"),
            P("row", "col"),
            P("row", None),
            P("col", None),
            P("row", "col"),
            P(("grp", "row")),
        ),
        out_specs=(P(("grp", "col"), "row"), P(("grp", "row"), "col"), P(("row", "col"), "grp")),
        check_vma=False,
    )
```

```python
import functools

import jax
import jax.numpy as jnp
from jax import lax
from jax.experimental import pallas as pl
from jax.experimental.pallas import tpu as pltpu
from jax.sharding import PartitionSpec as P

EXAMPLES = 8
CHUNKS = 4
KERNEL_CHUNKS = 4


def swap(x, axis, bit):
    n = lax.axis_size(axis)
    return lax.ppermute(x, axis, [(i, i ^ bit) for i in range(n)])


def pair_order(own, other, index, axis):
    first = jnp.where(index == 0, own, other)
    second = jnp.where(index == 0, other, own)
    return jnp.concatenate([first, second], axis=axis)


def gather_rows(block):
    n = lax.axis_size("row")
    if n % 2 or n > 16:
        return lax.all_gather(block, "row", axis=0, tiled=True)
    outer = n // 2
    me = lax.axis_index("row")
    z, x = me // 2, me % 2
    held = [block]
    for k in range(1, outer):
        perm = [(i, ((i // 2 + k) % outer) * 2 + i % 2) for i in range(n)]
        held.append(lax.ppermute(block, "row", perm))
    mine = jnp.stack(held[::-1])
    theirs = swap(mine, "row", 1)
    both = pair_order(mine, theirs, x, 1)
    twice = jnp.concatenate([both, both], axis=0)
    rows = lax.dynamic_slice_in_dim(twice, outer - 1 - z, outer, 0)
    return rows.reshape((n * block.shape[0],) + block.shape[1:])


def sum_rows(x):
    n = lax.axis_size("row")
    if n & (n - 1):
        return lax.psum(x, "row")
    bit = 1
    while bit < n:
        x = x + swap(x, "row", bit)
        bit *= 2
    return x


def product_kernel(a_ref, b_ref, *refs):
    out_ref = refs[-1]
    out_ref[...] = jnp.dot(
        a_ref[...], b_ref[...], preferred_element_type=jnp.float32
    ).astype(out_ref.dtype)


def product_into(a, b, total, at, chunks):
    rows, depth = a.shape
    width = b.shape[1]
    tile = rows
    for parts in (8, 4, 2):
        if rows % (parts * 16) == 0:
            tile = rows // parts
            break
    in_specs = [
        pl.BlockSpec((tile, depth), lambda i: (i, 0)),
        pl.BlockSpec((depth, width), lambda i: (0, 0)),
    ]
    args = (a, b)
    aliases = {}
    if total is not None:
        in_specs.append(pl.BlockSpec(memory_space=pl.ANY))
        args = (a, b, total)
        aliases = {2: 0}
    return pl.pallas_call(
        product_kernel,
        grid=(rows // tile,),
        in_specs=in_specs,
        out_specs=pl.BlockSpec((tile, width), lambda i: (i, at)),
        out_shape=jax.ShapeDtypeStruct((rows, chunks * width), jnp.bfloat16),
        input_output_aliases=aliases,
        compiler_params=pltpu.CompilerParams(vmem_limit_bytes=24 << 20),
        cost_estimate=pl.CostEstimate(
            flops=2 * rows * depth * width,
            bytes_accessed=2 * (rows * depth + depth * width + rows * width),
            transcendentals=0,
        ),
    )(*args)


def plain_body(grad_out, hidden_act, down_weight, proj_in, proj_out, queries, example_ids):
    f32 = jnp.float32
    col = lax.axis_index("col")
    half_rank = proj_in.shape[1] // lax.axis_size("col")

    width = grad_out.shape[1] // CHUNKS
    parts = [
        gather_rows(lax.slice_in_dim(grad_out, c * width, (c + 1) * width, axis=1))
        for c in range(CHUNKS)
    ]

    other_hidden = swap(hidden_act, "col", 1)
    full_hidden = pair_order(hidden_act, other_hidden, col, 0)
    hidden_t = full_hidden.T

    own_proj = lax.dynamic_slice_in_dim(proj_in, col * half_rank, half_rank, 1)
    in_factor = sum_rows(
        lax.dot_general(own_proj, full_hidden, (((0,), (1,)), ((), ())), preferred_element_type=f32)
    )

    out_own = lax.dot_general(
        proj_out, grad_out, (((0,), (1,)), ((), ())), preferred_element_type=f32
    ).T
    out_own = out_own + swap(out_own, "col", 1)
    packed = gather_rows(jnp.concatenate([out_own, example_ids[:, None].astype(f32)], axis=1))
    out_factor = packed[:, :-1]
    ids = packed[:, -1].astype(jnp.int32)
    labels = jnp.arange(EXAMPLES, dtype=jnp.int32)
    onehot = ids[None, :] == labels[:, None]
    masked = jnp.where(onehot[:, None, :], in_factor[None], 0.0)
    example_grads = jnp.dot(
        masked.reshape(EXAMPLES * half_rank, -1), out_factor, precision=lax.Precision.HIGHEST
    ).reshape(EXAMPLES, -1)
    values = lax.dot_general(
        queries.astype(f32), example_grads, (((1,), (1,)), ((), ())), precision=lax.Precision.HIGHEST
    )
    share = values.shape[0] // 2
    keep = lax.dynamic_slice_in_dim(values, col * share, share, 0)
    send = lax.dynamic_slice_in_dim(values, (1 - col) * share, share, 0)
    scores = keep + swap(send, "col", 1)

    total = None
    weight_grad = None
    for c in range(CHUNKS):
        weights = lax.slice_in_dim(down_weight, c * width, (c + 1) * width, axis=1)
        term = lax.dot_general(
            parts[c], weights, (((1,), (1,)), ((), ())), preferred_element_type=f32
        )
        total = term if total is None else total + term
        weight_grad = product_into(hidden_t, parts[c], weight_grad, c, CHUNKS)
    tokens = total.shape[0] // 2
    keep = lax.dynamic_slice_in_dim(total, col * tokens, tokens, 0)
    send = lax.dynamic_slice_in_dim(total, (1 - col) * tokens, tokens, 0)
    grad_hidden = (keep + swap(send, "col", 1)).astype(jnp.bfloat16)
    return (grad_hidden, weight_grad, scores)


def tiling(rows):
    for parts in (4, 2):
        if rows % (parts * 16) == 0:
            return rows // parts
    return rows


def row_ids(z, x):
    return z * 2 + x


def gather_kernel(
    n, chunks, g_ref, h_ref, w_ref, p_ref, q_ref, ids_ref,
    gh_ref, gall_ref, ht_ref, in_ref, out_ref,
    gbuf, wbuf, hbuf, acc, rbuf, sums, rsum, outs, rout,
    z_send, z_recv, x_send, x_recv, w_sem, own_sem, all_sem, h_sem, ht_sem,
    a_send, a_recv, s_send, s_recv, o_send, o_recv,
):
    f32 = jnp.float32
    me = lax.axis_index("row")
    col = lax.axis_index("col")
    outer = n // 2
    z, x = me // 2, me % 2
    tok = g_ref.shape[0]
    width = g_ref.shape[1] // chunks
    rows, half = h_ref.shape
    tile = tiling(rows)
    tiles = rows // tile
    partner = {"row": row_ids(z, 1 - x)}
    twin = {"col": 1 - col}
    mesh_ids = pl.DeviceIdType.MESH

    def ahead(k):
        return {"row": row_ids((z + k) % outer, x)}

    barrier = pltpu.get_barrier_semaphore()
    peers = [partner, twin] + [ahead(k) for k in range(1, outer)]
    for peer in peers:
        pl.semaphore_signal(barrier, inc=1, device_id=peer, device_id_type=mesh_ids)
    pl.semaphore_wait(barrier, len(peers))

    def remote(src, dst, send, recv, device):
        return pltpu.make_async_remote_copy(
            src_ref=src, dst_ref=dst, send_sem=send, recv_sem=recv,
            device_id=device, device_id_type=mesh_ids,
        )

    def slot(c, owner):
        return gbuf.at[c, pl.ds(pl.multiple_of(owner * tok, tok), tok), :]

    hidden_own = pltpu.make_async_copy(h_ref, hbuf.at[col], h_sem.at[0])
    hidden_out = remote(h_ref, hbuf.at[col], h_sem.at[1], h_sem.at[2], twin)
    hidden_out.start()
    hidden_own.start()
    z_copies, x_copies, w_copies, own_copies = {}, {}, [], []
    for c in range(chunks):
        block = g_ref.at[:, c * width:(c + 1) * width]
        for k in range(1, outer):
            z_copies[c, k] = remote(
                block, slot(c, me), z_send.at[c, k], z_recv.at[c, k], ahead(k)
            )
            z_copies[c, k].start()
        x_copies[c, 0] = remote(block, slot(c, me), x_send.at[c, 0], x_recv.at[c, 0], partner)
        if c == 0:
            x_copies[c, 0].start()
        own_copies.append(pltpu.make_async_copy(block, slot(c, me), own_sem.at[c]))
        own_copies[c].start()
    for c in range(chunks):
        w_copies.append(
            pltpu.make_async_copy(
                w_ref.at[:, c * width:(c + 1) * width], wbuf.at[c], w_sem.at[c]
            )
        )
        w_copies[c].start()

    hidden_own.wait()
    hidden_out.wait()
    ht_copy = pltpu.make_async_copy(hbuf, ht_ref, ht_sem.at[0])
    ht_copy.start()
    rank = p_ref.shape[0]
    for h in range(2):
        sums[0, :rank, h * half:(h + 1) * half] = jnp.dot(
            p_ref[...], hbuf[h], preferred_element_type=f32
        )
    sums[0, rank:, :] = ids_ref[...]

    rounds = n.bit_length() - 1

    def round_copy(r):
        device = partner
        if r:
            bit = 1 << (r - 1)
            flipped = z + bit - 2 * bit * ((z // bit) % 2)
            device = {"row": row_ids(flipped, x)}
        return remote(sums.at[r], rsum.at[r], s_send.at[r], s_recv.at[r], device)

    round_copies = [round_copy(r) for r in range(rounds)]
    round_copies[0].start()

    def finish_round(r):
        round_copies[r].wait()
        total = sums[r] + rsum[r]
        if r + 1 < rounds:
            sums[r + 1] = total
            round_copies[r + 1].start()
        else:
            in_ref[...] = total

    outs[...] = jnp.zeros_like(outs)
    exchange = [
        remote(
            acc.at[1 - col, t * tile:(t + 1) * tile, :], rbuf.at[t * tile:(t + 1) * tile, :],
            a_send.at[t], a_recv.at[t], twin,
        )
        for t in range(tiles)
    ]
    out_copy = remote(outs, rout, o_send.at[0], o_recv.at[0], twin)
    all_copies = []

    def process(c):
        last = c == chunks - 1
        w_copies[c].wait()
        own_copies[c].wait()
        for k in range(outer):
            x_copies[c, k].wait_recv()
        all_copies.append(pltpu.make_async_copy(gbuf.at[c], gall_ref.at[c], all_sem.at[c]))
        all_copies[c].start()
        outs[...] += lax.dot_general(
            q_ref[:, c * width:(c + 1) * width], gbuf[c],
            (((1,), (1,)), ((), ())), preferred_element_type=f32,
        )
        if last:
            out_copy.start()

        for which in (1 - col, col):
            tokens = gbuf[c, pl.ds(pl.multiple_of(which * half, half), half), :]

            def one(t, carry, which=which, tokens=tokens):
                at = pl.ds(pl.multiple_of(t * tile, 16), tile)
                term = lax.dot_general(
                    wbuf[c, at, :], tokens, (((1,), (1,)), ((), ())), preferred_element_type=f32
                )
                if c:
                    term = term + acc[which, at, :]
                acc[which, at, :] = term
                return carry

            if last and which is not col:
                for t in range(tiles):
                    one(t, 0)
                    exchange[t].start()
            else:
                lax.fori_loop(0, tiles, one, 0)

    for c in range(chunks):
        if c:
            x_copies[c, 0].start()
        for k in range(1, outer):
            z_copies[c, k].wait_recv()
            landed = slot(c, row_ids((z + outer - k) % outer, x))
            x_copies[c, k] = remote(landed, landed, x_send.at[c, k], x_recv.at[c, k], partner)
            x_copies[c, k].start()
        if c:
            process(c - 1)
        if c < rounds:
            finish_round(c)
    process(chunks - 1)
    for r in range(chunks, rounds):
        finish_round(r)

    out_copy.wait()
    out_ref[...] = outs[...] + rout[...]
    for t in range(tiles):
        exchange[t].wait()
        at = slice(t * tile, (t + 1) * tile)
        gh_ref[at, :] = (acc[col, at, :] + rbuf[at, :]).astype(gh_ref.dtype)
    for c in range(chunks):
        for k in range(outer):
            x_copies[c, k].wait_send()
            if k:
                z_copies[c, k].wait_send()
        all_copies[c].wait()
    ht_copy.wait()


def weight_kernel(h_ref, g_ref, out_ref):
    half = h_ref.shape[2]
    total = jnp.dot(h_ref[0], g_ref[0, :half, :], preferred_element_type=jnp.float32)
    total += jnp.dot(h_ref[1], g_ref[0, half:, :], preferred_element_type=jnp.float32)
    out_ref[...] = total.astype(out_ref.dtype)


def body(grad_out, hidden_act, down_weight, proj_in, proj_out, queries, example_ids):
    f32, bf16 = jnp.float32, jnp.bfloat16
    n = lax.axis_size("row")
    tok, features = grad_out.shape
    half, rows = hidden_act.shape
    if n & (n - 1) or n < 4 or n > 16 or lax.axis_size("col") != 2 or features % (128 * KERNEL_CHUNKS):
        return plain_body(
            grad_out, hidden_act, down_weight, proj_in, proj_out, queries, example_ids
        )
    chunks = KERNEL_CHUNKS
    col, row = lax.axis_index("col"), lax.axis_index("row")
    width = features // chunks
    tokens = n * tok
    rank = proj_in.shape[1]
    half_rank = rank // 2
    outer = n // 2
    rounds = n.bit_length() - 1
    tile = tiling(rows)
    tiles = rows // tile
    own_proj = lax.dynamic_slice_in_dim(proj_in.T, col * half_rank, half_rank, 0)
    own_ids = lax.dynamic_update_slice(
        jnp.zeros((8, tokens), f32),
        jnp.broadcast_to(example_ids.astype(f32)[None], (8, tok)),
        (0, row * tok),
    )
    anywhere = pl.BlockSpec(memory_space=pl.ANY)
    vmem = pl.BlockSpec(memory_space=pltpu.VMEM)
    dma = pltpu.SemaphoreType.DMA
    packed = half_rank + 8
    gh_t, grads, hidden_t, in_sum, out_sum = pl.pallas_call(
        functools.partial(gather_kernel, n, chunks),
        out_shape=(
            jax.ShapeDtypeStruct((rows, half), bf16),
            jax.ShapeDtypeStruct((chunks, tokens, width), bf16),
            jax.ShapeDtypeStruct((2, rows, half), bf16),
            jax.ShapeDtypeStruct((packed, tokens), f32),
            jax.ShapeDtypeStruct((rank, tokens), f32),
        ),
        in_specs=[anywhere, anywhere, anywhere, vmem, vmem, vmem],
        out_specs=(vmem, anywhere, anywhere, vmem, vmem),
        scratch_shapes=[
            pltpu.VMEM((chunks, tokens, width), bf16),
            pltpu.VMEM((chunks, rows, width), bf16),
            pltpu.VMEM((2, rows, half), bf16),
            pltpu.VMEM((2, rows, half), f32),
            pltpu.VMEM((rows, half), f32),
            pltpu.VMEM((rounds, packed, tokens), f32),
            pltpu.VMEM((rounds, packed, tokens), f32),
            pltpu.VMEM((rank, tokens), f32),
            pltpu.VMEM((rank, tokens), f32),
            dma((chunks, outer)), dma((chunks, outer)),
            dma((chunks, outer)), dma((chunks, outer)),
            dma((chunks,)), dma((chunks,)), dma((chunks,)), dma((3,)), dma((1,)),
            dma((tiles,)), dma((tiles,)), dma((rounds,)), dma((rounds,)), dma((1,)), dma((1,)),
        ],
        compiler_params=pltpu.CompilerParams(
            collective_id=0, has_side_effects=True, vmem_limit_bytes=56 << 20
        ),
        name="gather",
    )(grad_out, hidden_act.T, down_weight, own_proj, proj_out.T, own_ids)

    in_factor = in_sum[:half_rank]
    ids = in_sum[half_rank].astype(jnp.int32)
    labels = jnp.arange(EXAMPLES, dtype=jnp.int32)
    onehot = ids[None, :] == labels[:, None]
    masked = jnp.where(onehot[:, None, :], in_factor[None], 0.0)
    example_grads = lax.dot_general(
        masked.reshape(EXAMPLES * half_rank, -1), out_sum, (((1,), (1,)), ((), ())),
        precision=lax.Precision.HIGHEST,
    ).reshape(EXAMPLES, -1)
    values = lax.dot_general(
        queries.astype(f32), example_grads, (((1,), (1,)), ((), ())), precision=lax.Precision.HIGHEST
    )
    share = values.shape[0] // 2
    keep = lax.dynamic_slice_in_dim(values, col * share, share, 0)
    send = lax.dynamic_slice_in_dim(values, (1 - col) * share, share, 0)
    scores = keep + swap(send, "col", 1)

    weight_grad = pl.pallas_call(
        weight_kernel,
        grid=(chunks, tiles),
        in_specs=[
            pl.BlockSpec((2, tile, half), lambda c, t: (0, t, 0)),
            pl.BlockSpec((1, tokens, width), lambda c, t: (c, 0, 0)),
        ],
        out_specs=pl.BlockSpec((tile, width), lambda c, t: (t, c)),
        out_shape=jax.ShapeDtypeStruct((rows, features), bf16),
        compiler_params=pltpu.CompilerParams(vmem_limit_bytes=60 << 20),
        cost_estimate=pl.CostEstimate(
            flops=2 * rows * tokens * features,
            bytes_accessed=2 * (rows * tokens + tokens * features + rows * features),
            transcendentals=0,
        ),
        name="weight",
    )(hidden_t, grads)
    return (gh_t.T, weight_grad, scores)


def solution(mesh):
    return jax.shard_map(
        body,
        mesh=mesh,
        in_specs=(
            P(("grp", "row"), "col"),
            P(("grp", "col"), "row"),
            P("row", "col"),
            P("row", None),
            P("col", None),
            P("row", "col"),
            P(("grp", "row")),
        ),
        out_specs=(P(("grp", "col"), "row"), P(("grp", "row"), "col"), P(("row", "col"), "grp")),
        check_vma=False,
    )
```

```python
import functools

import jax
import jax.numpy as jnp
from jax import lax
from jax.experimental import pallas as pl
from jax.experimental.pallas import tpu as pltpu
from jax.sharding import PartitionSpec as P

EXAMPLES = 8
CHUNKS = 4
KERNEL_CHUNKS = 4


def swap(x, axis, bit):
    n = lax.axis_size(axis)
    return lax.ppermute(x, axis, [(i, i ^ bit) for i in range(n)])


def pair_order(own, other, index, axis):
    first = jnp.where(index == 0, own, other)
    second = jnp.where(index == 0, other, own)
    return jnp.concatenate([first, second], axis=axis)


def gather_rows(block):
    n = lax.axis_size("row")
    if n % 2 or n > 16:
        return lax.all_gather(block, "row", axis=0, tiled=True)
    outer = n // 2
    me = lax.axis_index("row")
    z, x = me // 2, me % 2
    held = [block]
    for k in range(1, outer):
        perm = [(i, ((i // 2 + k) % outer) * 2 + i % 2) for i in range(n)]
        held.append(lax.ppermute(block, "row", perm))
    mine = jnp.stack(held[::-1])
    theirs = swap(mine, "row", 1)
    both = pair_order(mine, theirs, x, 1)
    twice = jnp.concatenate([both, both], axis=0)
    rows = lax.dynamic_slice_in_dim(twice, outer - 1 - z, outer, 0)
    return rows.reshape((n * block.shape[0],) + block.shape[1:])


def sum_rows(x):
    n = lax.axis_size("row")
    if n & (n - 1):
        return lax.psum(x, "row")
    bit = 1
    while bit < n:
        x = x + swap(x, "row", bit)
        bit *= 2
    return x


def product_kernel(a_ref, b_ref, *refs):
    out_ref = refs[-1]
    out_ref[...] = jnp.dot(
        a_ref[...], b_ref[...], preferred_element_type=jnp.float32
    ).astype(out_ref.dtype)


def product_into(a, b, total, at, chunks):
    rows, depth = a.shape
    width = b.shape[1]
    tile = rows
    for parts in (8, 4, 2):
        if rows % (parts * 16) == 0:
            tile = rows // parts
            break
    in_specs = [
        pl.BlockSpec((tile, depth), lambda i: (i, 0)),
        pl.BlockSpec((depth, width), lambda i: (0, 0)),
    ]
    args = (a, b)
    aliases = {}
    if total is not None:
        in_specs.append(pl.BlockSpec(memory_space=pl.ANY))
        args = (a, b, total)
        aliases = {2: 0}
    return pl.pallas_call(
        product_kernel,
        grid=(rows // tile,),
        in_specs=in_specs,
        out_specs=pl.BlockSpec((tile, width), lambda i: (i, at)),
        out_shape=jax.ShapeDtypeStruct((rows, chunks * width), jnp.bfloat16),
        input_output_aliases=aliases,
        compiler_params=pltpu.CompilerParams(vmem_limit_bytes=24 << 20),
        cost_estimate=pl.CostEstimate(
            flops=2 * rows * depth * width,
            bytes_accessed=2 * (rows * depth + depth * width + rows * width),
            transcendentals=0,
        ),
    )(*args)


def plain_body(grad_out, hidden_act, down_weight, proj_in, proj_out, queries, example_ids):
    f32 = jnp.float32
    col = lax.axis_index("col")
    half_rank = proj_in.shape[1] // lax.axis_size("col")

    width = grad_out.shape[1] // CHUNKS
    parts = [
        gather_rows(lax.slice_in_dim(grad_out, c * width, (c + 1) * width, axis=1))
        for c in range(CHUNKS)
    ]

    other_hidden = swap(hidden_act, "col", 1)
    full_hidden = pair_order(hidden_act, other_hidden, col, 0)
    hidden_t = full_hidden.T

    own_proj = lax.dynamic_slice_in_dim(proj_in, col * half_rank, half_rank, 1)
    in_factor = sum_rows(
        lax.dot_general(own_proj, full_hidden, (((0,), (1,)), ((), ())), preferred_element_type=f32)
    )

    out_own = lax.dot_general(
        proj_out, grad_out, (((0,), (1,)), ((), ())), preferred_element_type=f32
    ).T
    out_own = out_own + swap(out_own, "col", 1)
    packed = gather_rows(jnp.concatenate([out_own, example_ids[:, None].astype(f32)], axis=1))
    out_factor = packed[:, :-1]
    ids = packed[:, -1].astype(jnp.int32)
    labels = jnp.arange(EXAMPLES, dtype=jnp.int32)
    onehot = ids[None, :] == labels[:, None]
    masked = jnp.where(onehot[:, None, :], in_factor[None], 0.0)
    example_grads = jnp.dot(
        masked.reshape(EXAMPLES * half_rank, -1), out_factor, precision=lax.Precision.HIGHEST
    ).reshape(EXAMPLES, -1)
    values = lax.dot_general(
        queries.astype(f32), example_grads, (((1,), (1,)), ((), ())), precision=lax.Precision.HIGHEST
    )
    share = values.shape[0] // 2
    keep = lax.dynamic_slice_in_dim(values, col * share, share, 0)
    send = lax.dynamic_slice_in_dim(values, (1 - col) * share, share, 0)
    scores = keep + swap(send, "col", 1)

    total = None
    weight_grad = None
    for c in range(CHUNKS):
        weights = lax.slice_in_dim(down_weight, c * width, (c + 1) * width, axis=1)
        term = lax.dot_general(
            parts[c], weights, (((1,), (1,)), ((), ())), preferred_element_type=f32
        )
        total = term if total is None else total + term
        weight_grad = product_into(hidden_t, parts[c], weight_grad, c, CHUNKS)
    tokens = total.shape[0] // 2
    keep = lax.dynamic_slice_in_dim(total, col * tokens, tokens, 0)
    send = lax.dynamic_slice_in_dim(total, (1 - col) * tokens, tokens, 0)
    grad_hidden = (keep + swap(send, "col", 1)).astype(jnp.bfloat16)
    return (grad_hidden, weight_grad, scores)


def tiling(rows):
    for parts in (4, 2):
        if rows % (parts * 16) == 0:
            return rows // parts
    return rows


def row_ids(z, x):
    return z * 2 + x


def gather_kernel(
    n, chunks, g_ref, h_ref, w_ref, p_ref, q_ref, ids_ref,
    gh_ref, gall_ref, ht_ref, in_ref, out_ref,
    gbuf, wbuf, hbuf, acc, rbuf, sums, rsum, outs, rout,
    z_send, z_recv, x_send, x_recv, w_sem, own_sem, all_sem, h_sem, ht_sem,
    a_send, a_recv, s_send, s_recv, o_send, o_recv,
):
    f32 = jnp.float32
    me = lax.axis_index("row")
    col = lax.axis_index("col")
    outer = n // 2
    z, x = me // 2, me % 2
    tok = g_ref.shape[0]
    width = g_ref.shape[1] // chunks
    rows, half = h_ref.shape
    tile = tiling(rows)
    tiles = rows // tile
    partner = {"row": row_ids(z, 1 - x)}
    twin = {"col": 1 - col}
    mesh_ids = pl.DeviceIdType.MESH

    def ahead(k):
        return {"row": row_ids((z + k) % outer, x)}

    barrier = pltpu.get_barrier_semaphore()
    peers = [partner, twin] + [ahead(k) for k in range(1, outer)]
    for peer in peers:
        pl.semaphore_signal(barrier, inc=1, device_id=peer, device_id_type=mesh_ids)
    pl.semaphore_wait(barrier, len(peers))

    def remote(src, dst, send, recv, device):
        return pltpu.make_async_remote_copy(
            src_ref=src, dst_ref=dst, send_sem=send, recv_sem=recv,
            device_id=device, device_id_type=mesh_ids,
        )

    def slot(c, owner):
        return gbuf.at[c, pl.ds(pl.multiple_of(owner * tok, tok), tok), :]

    hidden_own = pltpu.make_async_copy(h_ref, hbuf.at[col], h_sem.at[0])
    hidden_out = remote(h_ref, hbuf.at[col], h_sem.at[1], h_sem.at[2], twin)
    hidden_out.start()
    hidden_own.start()
    z_copies, x_copies, w_copies, own_copies = {}, {}, [], []
    for c in range(chunks):
        block = g_ref.at[:, c * width:(c + 1) * width]
        for k in range(1, outer):
            z_copies[c, k] = remote(
                block, slot(c, me), z_send.at[c, k], z_recv.at[c, k], ahead(k)
            )
            z_copies[c, k].start()
        x_copies[c, 0] = remote(block, slot(c, me), x_send.at[c, 0], x_recv.at[c, 0], partner)
        if c == 0:
            x_copies[c, 0].start()
        own_copies.append(pltpu.make_async_copy(block, slot(c, me), own_sem.at[c]))
        own_copies[c].start()
    for c in range(chunks):
        w_copies.append(
            pltpu.make_async_copy(
                w_ref.at[:, c * width:(c + 1) * width], wbuf.at[c], w_sem.at[c]
            )
        )
        w_copies[c].start()

    hidden_own.wait()
    hidden_out.wait()
    ht_copies = [
        pltpu.make_async_copy(hbuf.at[h], ht_ref.at[:, h * half:(h + 1) * half], ht_sem.at[h])
        for h in range(2)
    ]
    for copy in ht_copies:
        copy.start()
    rank = p_ref.shape[0]
    for h in range(2):
        sums[0, :rank, h * half:(h + 1) * half] = jnp.dot(
            p_ref[...], hbuf[h], preferred_element_type=f32
        )
    sums[0, rank:, :] = ids_ref[...]

    rounds = n.bit_length() - 1

    def round_copy(r):
        device = partner
        if r:
            bit = 1 << (r - 1)
            flipped = z + bit - 2 * bit * ((z // bit) % 2)
            device = {"row": row_ids(flipped, x)}
        return remote(sums.at[r], rsum.at[r], s_send.at[r], s_recv.at[r], device)

    round_copies = [round_copy(r) for r in range(rounds)]
    round_copies[0].start()

    def finish_round(r):
        round_copies[r].wait()
        total = sums[r] + rsum[r]
        if r + 1 < rounds:
            sums[r + 1] = total
            round_copies[r + 1].start()
        else:
            in_ref[...] = total

    outs[...] = jnp.zeros_like(outs)
    exchange = [
        remote(
            acc.at[1 - col, t * tile:(t + 1) * tile, :], rbuf.at[t * tile:(t + 1) * tile, :],
            a_send.at[t], a_recv.at[t], twin,
        )
        for t in range(tiles)
    ]
    out_copy = remote(outs, rout, o_send.at[0], o_recv.at[0], twin)
    all_copies = []

    def process(c):
        last = c == chunks - 1
        w_copies[c].wait()
        own_copies[c].wait()
        for k in range(outer):
            x_copies[c, k].wait_recv()
        all_copies.append(pltpu.make_async_copy(gbuf.at[c], gall_ref.at[c], all_sem.at[c]))
        all_copies[c].start()
        outs[...] += lax.dot_general(
            q_ref[:, c * width:(c + 1) * width], gbuf[c],
            (((1,), (1,)), ((), ())), preferred_element_type=f32,
        )
        if last:
            out_copy.start()

        for which in (1 - col, col):
            tokens = gbuf[c, pl.ds(pl.multiple_of(which * half, half), half), :]

            def one(t, carry, which=which, tokens=tokens):
                at = pl.ds(pl.multiple_of(t * tile, 16), tile)
                term = lax.dot_general(
                    wbuf[c, at, :], tokens, (((1,), (1,)), ((), ())), preferred_element_type=f32
                )
                if c:
                    term = term + acc[which, at, :]
                acc[which, at, :] = term
                return carry

            if last and which is not col:
                for t in range(tiles):
                    one(t, 0)
                    exchange[t].start()
            else:
                lax.fori_loop(0, tiles, one, 0)

    for c in range(chunks):
        if c:
            x_copies[c, 0].start()
        for k in range(1, outer):
            z_copies[c, k].wait_recv()
            landed = slot(c, row_ids((z + outer - k) % outer, x))
            x_copies[c, k] = remote(landed, landed, x_send.at[c, k], x_recv.at[c, k], partner)
            x_copies[c, k].start()
        if c:
            process(c - 1)
        if c < rounds:
            finish_round(c)
    process(chunks - 1)
    for r in range(chunks, rounds):
        finish_round(r)

    out_copy.wait()
    out_ref[...] = outs[...] + rout[...]
    for t in range(tiles):
        exchange[t].wait()
        at = slice(t * tile, (t + 1) * tile)
        gh_ref[at, :] = (acc[col, at, :] + rbuf[at, :]).astype(gh_ref.dtype)
    for c in range(chunks):
        for k in range(outer):
            x_copies[c, k].wait_send()
            if k:
                z_copies[c, k].wait_send()
        all_copies[c].wait()
    for copy in ht_copies:
        copy.wait()


def weight_kernel(h_ref, g_ref, out_ref):
    total = jnp.dot(h_ref[...], g_ref[0], preferred_element_type=jnp.float32)
    out_ref[...] = total.astype(out_ref.dtype)


def body(grad_out, hidden_act, down_weight, proj_in, proj_out, queries, example_ids):
    f32, bf16 = jnp.float32, jnp.bfloat16
    n = lax.axis_size("row")
    tok, features = grad_out.shape
    half, rows = hidden_act.shape
    if n & (n - 1) or n < 4 or n > 16 or lax.axis_size("col") != 2 or features % (128 * KERNEL_CHUNKS):
        return plain_body(
            grad_out, hidden_act, down_weight, proj_in, proj_out, queries, example_ids
        )
    chunks = KERNEL_CHUNKS
    col, row = lax.axis_index("col"), lax.axis_index("row")
    width = features // chunks
    tokens = n * tok
    rank = proj_in.shape[1]
    half_rank = rank // 2
    outer = n // 2
    rounds = n.bit_length() - 1
    tile = tiling(rows)
    tiles = rows // tile
    own_proj = lax.dynamic_slice_in_dim(proj_in.T, col * half_rank, half_rank, 0)
    own_ids = lax.dynamic_update_slice(
        jnp.zeros((8, tokens), f32),
        jnp.broadcast_to(example_ids.astype(f32)[None], (8, tok)),
        (0, row * tok),
    )
    anywhere = pl.BlockSpec(memory_space=pl.ANY)
    vmem = pl.BlockSpec(memory_space=pltpu.VMEM)
    dma = pltpu.SemaphoreType.DMA
    packed = half_rank + 8
    gh_t, grads, hidden_t, in_sum, out_sum = pl.pallas_call(
        functools.partial(gather_kernel, n, chunks),
        out_shape=(
            jax.ShapeDtypeStruct((rows, half), bf16),
            jax.ShapeDtypeStruct((chunks, tokens, width), bf16),
            jax.ShapeDtypeStruct((rows, 2 * half), bf16),
            jax.ShapeDtypeStruct((packed, tokens), f32),
            jax.ShapeDtypeStruct((rank, tokens), f32),
        ),
        in_specs=[anywhere, anywhere, anywhere, vmem, vmem, vmem],
        out_specs=(vmem, anywhere, anywhere, vmem, vmem),
        scratch_shapes=[
            pltpu.VMEM((chunks, tokens, width), bf16),
            pltpu.VMEM((chunks, rows, width), bf16),
            pltpu.VMEM((2, rows, half), bf16),
            pltpu.VMEM((2, rows, half), f32),
            pltpu.VMEM((rows, half), f32),
            pltpu.VMEM((rounds, packed, tokens), f32),
            pltpu.VMEM((rounds, packed, tokens), f32),
            pltpu.VMEM((rank, tokens), f32),
            pltpu.VMEM((rank, tokens), f32),
            dma((chunks, outer)), dma((chunks, outer)),
            dma((chunks, outer)), dma((chunks, outer)),
            dma((chunks,)), dma((chunks,)), dma((chunks,)), dma((3,)), dma((2,)),
            dma((tiles,)), dma((tiles,)), dma((rounds,)), dma((rounds,)), dma((1,)), dma((1,)),
        ],
        compiler_params=pltpu.CompilerParams(
            collective_id=0, has_side_effects=True, vmem_limit_bytes=56 << 20
        ),
        name="gather",
    )(grad_out, hidden_act.T, down_weight, own_proj, proj_out.T, own_ids)

    in_factor = in_sum[:half_rank]
    ids = in_sum[half_rank].astype(jnp.int32)
    labels = jnp.arange(EXAMPLES, dtype=jnp.int32)
    onehot = ids[None, :] == labels[:, None]
    masked = jnp.where(onehot[:, None, :], in_factor[None], 0.0)
    example_grads = lax.dot_general(
        masked.reshape(EXAMPLES * half_rank, -1), out_sum, (((1,), (1,)), ((), ())),
        precision=lax.Precision.HIGHEST,
    ).reshape(EXAMPLES, -1)
    values = lax.dot_general(
        queries.astype(f32), example_grads, (((1,), (1,)), ((), ())), precision=lax.Precision.HIGHEST
    )
    share = values.shape[0] // 2
    keep = lax.dynamic_slice_in_dim(values, col * share, share, 0)
    send = lax.dynamic_slice_in_dim(values, (1 - col) * share, share, 0)
    scores = keep + swap(send, "col", 1)

    weight_grad = pl.pallas_call(
        weight_kernel,
        grid=(chunks, tiles),
        in_specs=[
            pl.BlockSpec((tile, 2 * half), lambda c, t: (t, 0)),
            pl.BlockSpec((1, tokens, width), lambda c, t: (c, 0, 0)),
        ],
        out_specs=pl.BlockSpec((tile, width), lambda c, t: (t, c)),
        out_shape=jax.ShapeDtypeStruct((rows, features), bf16),
        compiler_params=pltpu.CompilerParams(vmem_limit_bytes=60 << 20),
        cost_estimate=pl.CostEstimate(
            flops=2 * rows * tokens * features,
            bytes_accessed=2 * (rows * tokens + tokens * features + rows * features),
            transcendentals=0,
        ),
        name="weight",
    )(hidden_t, grads)
    return (gh_t.T, weight_grad, scores)


def solution(mesh):
    return jax.shard_map(
        body,
        mesh=mesh,
        in_specs=(
            P(("grp", "row"), "col"),
            P(("grp", "col"), "row"),
            P("row", "col"),
            P("row", None),
            P("col", None),
            P("row", "col"),
            P(("grp", "row")),
        ),
        out_specs=(P(("grp", "col"), "row"), P(("grp", "row"), "col"), P(("row", "col"), "grp")),
        check_vma=False,
    )
```
